32 devices in a mesh: groups: 2 (over y), chan: 4 (over z), win: 2 (over x), sub: 2 (over core).
Axes of the slice: x: 2, y: 2, z: 4, core: 2. Of those that a mesh axis runs over, the one named last changes fastest.
Arguments:
- traces: bfloat16 [4, 2560, 1024], P(('groups', 'win'), 'chan'), parts along dimension 0, may hold values from -240 to 240, as said below
- channel_mask: int32 [5120], P(('groups', 'chan')), parts along dimension 0, may hold values 0 or 1
- smooth_width: int32 [512], replicated, may hold values from 1 to 16, as said below
- source_phase: int32 [8], P('groups'), parts along dimension 0, may hold values from 0 to 7
- pair_list: int32 [8, 5], P('groups'), parts along dimension 0, may hold values 0 or 1
Outputs:
- receiver_stack: float32 [8, 5, 101, 5120], P(('win', 'sub'), None, None, ('groups', 'chan')), parts along dimension 3
- source_stack: float32 [64, 5, 101, 640], P(('groups', 'chan', 'win', 'sub')), parts along dimension 0
The draws below stay inside these ranges and needn't reach their ends.
There are 2 independent parts, one for each index of `groups`. The reference program is written for one: setup_inputs(seed, part) draws one part's arguments, and reference() takes and returns one part's arrays. A program takes and returns all parts, laid end to end along the dimension named above; an argument that names none is the same for every part. Nothing has to cross between parts.
Inputs may be any that keep to these rules, and one draw needn't show every extreme that they name: `traces`: float samples; each channel and each window has a scale of its own. `smooth_width`: every value from 1 to 16 may occur; 16 occurs in every draw.
All inputs are finite; a program needn't handle non-finite values. No bound on the sum of `channel_mask` on one device may be relied on, other than what follows from the above.
Results may differ from the reference program's by a relative error of at most 0.0052.
Values may be sent and summed in bfloat16 or wider, within the bound.
A program may use at most 192 MiB of HBM per device.

```python
import math
import jax
import jax.numpy as jnp
from jax import lax

NB = 512
MAXLAG = 50
STRIDE = 8
SMAX = 16
REACH = 2
CB = 640
VS = 8
LSAMP = 1024
LAGS = 101
OFFS = 5
NBLK = 4
NCH = 2560
NSRC = 32
WINDOWS = 2


def draw_traces(key, part):
    k_noise, k_chan, k_win = jax.random.split(key, 3)
    chan_scale = jnp.exp(jax.random.uniform(k_chan, (NCH,), jnp.float32, 0.0, math.log(10.0)))
    win_scale = jnp.exp(jax.random.uniform(k_win, (WINDOWS,), jnp.float32, 0.0, math.log(4.0)))
    noise_draw = jnp.clip(jax.random.normal(k_noise, (WINDOWS, NCH, LSAMP), jnp.float32), -6.0, 6.0)
    return (noise_draw * chan_scale[None, :, None] * win_scale[:, None, None]).astype(jnp.bfloat16)


def draw_smooth_width(key, part):
    k_vals, k_pos = jax.random.split(jax.random.fold_in(key, 17))
    widths = jax.random.randint(k_vals, (NB,), 1, SMAX + 1)
    spot_ids = jax.random.randint(k_pos, (2,), 0, NB)
    bin_ids = jnp.arange(NB)
    widths = jnp.where(bin_ids == spot_ids[0], SMAX, widths)
    widths = jnp.where((bin_ids == spot_ids[1]) & (bin_ids != spot_ids[0]), 1, widths)
    return widths.astype(jnp.int32)


def place_ends(entries, stream_key, least, largest):
    place = [jax.random.randint(jax.random.fold_in(stream_key, axis), (), 0, length) for axis, length in enumerate(entries.shape)]
    main_axis = entries.shape.index(max(entries.shape))
    neighbour = place[:main_axis] + [(place[main_axis] + 1) % entries.shape[main_axis]] + place[main_axis + 1:]
    return entries.at[tuple(place)].set(least).at[tuple(neighbour)].set(largest)


def setup_inputs(seed: int = 0, part: int = 0) -> dict:
    keys = jax.random.split(jax.random.key(seed), 6)
    own_keys = jax.random.split(jax.random.fold_in(keys[5], part), 6)
    return {
        "traces": draw_traces(jax.random.fold_in(jax.random.fold_in(keys[5], part), 71), part),
        "channel_mask": place_ends((jax.random.randint(own_keys[1], (NCH,), 0, 8) < 7).astype(jnp.int32), jax.random.fold_in(own_keys[1], 1), 0, 1),
        "smooth_width": draw_smooth_width(jax.random.fold_in(keys[5], 71), part),
        "source_phase": place_ends(jax.random.randint(own_keys[3], (NBLK,), 0, STRIDE), jax.random.fold_in(own_keys[3], 1), 0, STRIDE - 1).astype(jnp.int32),
        "pair_list": place_ends((jax.random.randint(own_keys[4], (NBLK, OFFS), 0, 4) < 3).astype(jnp.int32), jax.random.fold_in(own_keys[4], 1), 0, 1),
    }


FLOOR = 0.25

def dft_tables(samples, bin_ids):
    sample_ids = jnp.arange(samples, dtype=jnp.int32)
    phases = sample_ids[:, None] * bin_ids[None, :] % samples
    angles = phases.astype(jnp.float32) * (2.0 * math.pi / samples)
    return jnp.concatenate([jnp.cos(angles), -jnp.sin(angles)], axis=1)

def lag_tables(samples, bin_ids, maxlag):
    lag_ids = jnp.arange(2 * maxlag + 1, dtype=jnp.int32) - maxlag
    phases = lag_ids[:, None] * bin_ids[None, :] % samples
    angles = phases.astype(jnp.float32) * (2.0 * math.pi / samples)
    return jnp.stack([jnp.cos(angles), -jnp.sin(angles)], axis=1)

def smoothing_weights(row_ids, bin_ids, widths, bin_total):
    nearby = jnp.abs(row_ids[:, None] - bin_ids[None, :]) <= widths[None, :]
    inside = (row_ids >= 0) & (row_ids < bin_total)
    return jnp.where(nearby & inside[:, None], 1.0, 0.0).astype(jnp.float32)

def cross_lags(sources, spectra, lag_tab):
    turned = jnp.stack([sources[:, 1], -sources[:, 0]], axis=1)
    stacked_pair = jnp.stack([sources, turned], axis=0)
    cross_spec = jnp.einsum('pwqvk,wqkc->pkvc', stacked_pair, spectra, precision=lax.Precision.HIGHEST)
    return jnp.einsum('tpk,pkvc->vtc', lag_tab, cross_spec, precision=lax.Precision.HIGHEST)

def reference(traces, channel_mask, smooth_width, source_phase, pair_list):
    bin_ids = jnp.arange(NB, dtype=jnp.int32)
    tables = dft_tables(LSAMP, bin_ids).astype(jnp.bfloat16)
    tables = lax.optimization_barrier(tables).astype(jnp.float32)
    spectrum = jnp.einsum('wcn,nk->wkc', traces.astype(jnp.float32), tables, precision=lax.Precision.HIGHEST) * LSAMP ** (-0.5)
    spectrum = spectrum * channel_mask.astype(jnp.float32)[None, None, :]
    spectrum = spectrum.reshape(WINDOWS, 2, NB, NCH)
    amplitude = jnp.sqrt(spectrum[:, 0] ** 2 + spectrum[:, 1] ** 2)
    weights = smoothing_weights(bin_ids, bin_ids, smooth_width, NB)
    smoothed = jnp.einsum('wjc,jk->wkc', amplitude, weights, precision=lax.Precision.HIGHEST) / lax.optimization_barrier(jnp.sum(weights, axis=0))[None, :, None]
    whitened = (spectrum / jnp.maximum(smoothed, FLOOR)[:, None]).astype(jnp.bfloat16)
    white_full = lax.optimization_barrier(whitened).astype(jnp.float32)
    grouped = white_full.reshape(WINDOWS, 2, NB, NBLK, CB // STRIDE, STRIDE)[:, :, :, :, :VS]
    picker = jnp.where(jnp.arange(STRIDE, dtype=jnp.int32)[None, :] == source_phase[:, None], 1.0, 0.0).astype(jnp.float32)
    sources = jnp.einsum('wqkbvs,bs->bwqvk', grouped, picker, precision=lax.Precision.HIGHEST)
    receivers = jnp.transpose(white_full.reshape(WINDOWS, 2, NB, NBLK, CB), (3, 0, 1, 2, 4))
    lag_tab = lag_tables(LSAMP, bin_ids, MAXLAG)
    factor = (NB * WINDOWS) ** (-0.5)
    stacks = []
    for offset in range(OFFS):
        moved_by = offset - REACH
        moved = jnp.roll(sources, moved_by, axis=0)
        paired = jnp.roll(pair_list[:, offset], moved_by).astype(jnp.float32)

        def one_block(block_items):
            return cross_lags(block_items[0], block_items[1], lag_tab) * block_items[2]
        lags_block = lax.map(one_block, (moved, receivers, paired))
        stacks.append(lags_block * factor)
    stacked = jnp.stack(stacks, axis=0)
    receiver_stack = jnp.transpose(stacked, (2, 0, 3, 1, 4)).reshape(VS, OFFS, LAGS, NCH)
    turned_back = []
    for offset in range(OFFS):
        moved_by = offset - REACH
        turned_back.append(jnp.flip(jnp.roll(stacked[offset], -moved_by, axis=0), axis=2))
    source_stack = jnp.transpose(jnp.stack(turned_back, axis=0), (1, 2, 0, 3, 4)).reshape(NSRC, OFFS, LAGS, CB)
    return (receiver_stack, source_stack)
```

```python
import functools
import math

import jax
import jax.numpy as jnp
import numpy as np
from jax import lax
from jax.experimental import pallas as pl
from jax.experimental.pallas import tpu as pltpu
from jax.sharding import PartitionSpec as P

NB = 512
MAXLAG = 50
LAGS = 2 * MAXLAG + 1
STRIDE = 8
REACH = 2
VS = 8
OFFS = 2 * REACH + 1
FLOOR = 0.25
TILE = 128
SPAN = 64
MESH = pl.DeviceIdType.MESH
FAR = (((1,), (1,)), ((), ()))


def dft_columns(samples):
    phases = np.arange(samples)[:, None] * np.arange(NB)[None, :] % samples
    angles = phases * (2.0 * math.pi / samples)
    return jnp.asarray(np.concatenate([np.cos(angles), -np.sin(angles)], axis=1), jnp.bfloat16)


def half_rows(mine):
    return -(-(MAXLAG + 1) * mine // 8) * 8


def lag_rows(samples, mine, factor):
    lags = np.arange(half_rows(mine)) // mine
    angles = (lags[:, None] * np.arange(NB) % samples) * (2.0 * math.pi / samples)
    return jnp.asarray(np.stack([np.cos(angles), np.sin(angles)]) * factor, jnp.float32)


def block_keys(blocks):
    keys = [0]
    for offset in range(OFFS):
        key = (offset - REACH) % blocks
        if key not in keys:
            keys.append(key)
    return keys


class Ring:
    def __init__(self, blocks, at):
        self.blocks, self.at = blocks, at
        self.keys = block_keys(blocks)
        self.paired = blocks == 4
        self.slots = len(self.keys)

    def taker(self, slot):
        if self.paired:
            odd = self.at % 2
            return [self.at, (self.at + 2) % 4, 3 - self.at, self.at + 1 - 2 * odd][slot]
        return lax.rem(self.at + self.keys[slot], self.blocks)

    def giver(self, slot):
        if self.paired:
            return self.taker(slot)
        return lax.rem(self.at + self.blocks - self.keys[slot], self.blocks)

    def source_slot(self, offset):
        step = offset - REACH
        if self.paired and step % 2:
            odd = self.at % 2
            return 3 - odd if step == -1 else 2 + odd
        return self.keys.index(step % self.blocks)

    def receiver_slot(self, offset):
        step = offset - REACH
        if self.paired and step % 2:
            odd = self.at % 2
            return 2 + odd if step == -1 else 3 - odd
        return self.keys.index(step % self.blocks)


def kernel(wins, subs, mine, tiles, phase_ref, pairs, traces, mask, widths, dft_hbm, lag_hbm,
           fwd, back,
           dft, lag, weights, span_raw, raw, other_raw, spectra, rows, staged, near, far,
           live, picked, flat, own_pack, packs, got,
           l_sem, x_send, x_recv, s_send, s_recv, n_send, n_recv, z_send, z_recv):
    samples = traces.shape[1]
    blocks = lax.axis_size("chan")
    block_at = lax.axis_index("chan")
    win_at = lax.axis_index("win")
    sub_at = lax.axis_index("sub")
    ring = Ring(blocks, block_at)
    slots = ring.slots
    per = -(-tiles // subs)
    half = TILE // subs
    chip = mine * subs
    hb = half_rows(mine)
    depth = 2 * NB

    def turned(d):
        return lax.rem(win_at + d, wins)

    barrier = pltpu.get_barrier_semaphore()
    greeted = 0
    for n in range(slots):
        for d in range(wins):
            for u in range(subs):
                if (n, d, u) != (0, 0, 0) and 0 in (n, d, u):
                    where = {"chan": ring.taker(n), "win": turned(d), "sub": lax.rem(sub_at + u, subs)}
                    pl.semaphore_signal(barrier, inc=1, device_id=where, device_id_type=MESH)
                    greeted += 1

    def tile_of(i):
        return sub_at * per + i

    loads = [
        pltpu.make_async_copy(traces.at[:SPAN], span_raw, l_sem.at[0]),
        pltpu.make_async_copy(dft_hbm, dft, l_sem.at[1]),
    ]
    for i in range(per):
        start = pl.multiple_of(jnp.minimum(tile_of(i), tiles - 1) * TILE, TILE)
        loads.append(pltpu.make_async_copy(traces.at[pl.ds(start, TILE)], raw.at[i], l_sem.at[2 + i]))
    loads.append(pltpu.make_async_copy(lag_hbm, lag, l_sem.at[2 + per]))
    for load in loads:
        load.start()

    width_row = widths[...].astype(jnp.float32)
    at = lax.broadcasted_iota(jnp.int32, (NB, NB), 0)
    to = lax.broadcasted_iota(jnp.int32, (NB, NB), 1)
    close = jnp.abs(at - to).astype(jnp.float32) <= width_row
    weights[...] = jnp.where(close, 1.0, 0.0).astype(jnp.bfloat16)
    bins = lax.broadcasted_iota(jnp.int32, (1, NB), 1).astype(jnp.float32)
    inside = jnp.minimum(bins + width_row, NB - 1.0) - jnp.maximum(bins - width_row, 0.0) + 1.0
    share = 1.0 / inside
    floor = FLOOR * samples**0.5

    def whiten(cut):
        both = jnp.dot(cut, dft[...], preferred_element_type=jnp.float32)
        re, im = both[:, :NB], both[:, NB:]
        amplitude = jnp.sqrt(re * re + im * im)
        high = amplitude.astype(jnp.bfloat16)
        low = (amplitude - high.astype(jnp.float32)).astype(jnp.bfloat16)
        total = jnp.dot(high, weights[...], preferred_element_type=jnp.float32)
        total = total + jnp.dot(low, weights[...], preferred_element_type=jnp.float32)
        gain = 1.0 / jnp.maximum(total * share, floor)
        return (re * gain).astype(jnp.bfloat16), (im * gain).astype(jnp.bfloat16)

    order = [(i, o) for i in range(per) for o in range(subs) if o * per + i < min((o + 1) * per, tiles)]

    def x_copy(i, o, d, s):
        start = pl.multiple_of((o * per + i) * TILE + s * half, half)
        return pltpu.make_async_remote_copy(
            src_ref=traces.at[pl.ds(start, half)],
            dst_ref=other_raw.at[d - 1, i, pl.ds(pl.multiple_of(s * half, half), half)],
            send_sem=x_send.at[i, o, d - 1], recv_sem=x_recv.at[i, d - 1, s],
            device_id={"win": turned(d), "sub": o}, device_id_type=MESH)

    x_copies = [[x_copy(i, o, d, sub_at) for d in range(1, wins)] for i, o in order]
    pl.semaphore_wait(barrier, greeted)
    for copy in x_copies[0]:
        copy.start()

    loads[0].wait()
    loads[1].wait()
    span_re, span_im = whiten(span_raw[...])
    phase = phase_ref[block_at]
    row_ids = lax.broadcasted_iota(jnp.int32, (VS, SPAN), 0)
    lane_ids = lax.broadcasted_iota(jnp.int32, (VS, SPAN), 1)
    alive = mask[:SPAN].reshape(1, SPAN).astype(jnp.float32)
    picker = jnp.where(lane_ids == phase + STRIDE * row_ids, alive, 0.0).astype(jnp.bfloat16)
    picked[:, :NB] = jnp.dot(picker, span_re, preferred_element_type=jnp.float32)
    picked[:, NB:] = jnp.dot(picker, span_im, preferred_element_type=jnp.float32)
    piece = packs.shape[-1]
    pieces = depth // piece
    for w in range(wins):
        for j in range(pieces):
            flat[w, j * chip : (j + 1) * chip, :] = picked[
                w * chip : (w + 1) * chip, j * piece : (j + 1) * piece]
    packs[...] = flat[...].astype(jnp.bfloat16)
    own_pack[...] = packs[win_at]
    s_copies = {}
    for n in list(range(1, slots)) + [0]:
        for d in range(wins):
            if (n, d) != (0, 0):
                s_copies[n, d] = pltpu.make_async_remote_copy(
                    src_ref=packs.at[turned(d)], dst_ref=got.at[n, d],
                    send_sem=s_send.at[n, d], recv_sem=s_recv.at[n, d],
                    device_id={"chan": ring.taker(n), "win": turned(d)}, device_id_type=MESH)
                s_copies[n, d].start()
    for copies in x_copies[1:]:
        for copy in copies:
            copy.start()

    def own_window(i):
        re, im = whiten(raw[i])
        spectra[i, :, :NB] = re
        spectra[i, :, NB:depth] = im

    def other_windows(i):
        for d in range(1, wins):
            for s in range(subs):
                x_copy(i, 0, d, s).wait_recv()
            re, im = whiten(other_raw[d - 1, i])
            spectra[i, :, d * depth : d * depth + NB] = re
            spectra[i, :, d * depth + NB : (d + 1) * depth] = im

    def fill(n):
        for d in range(wins):
            if (n, d) == (0, 0):
                pack = own_pack[...].astype(jnp.float32)
            else:
                s_copies[n, d].wait_recv()
                pack = got[n, d].astype(jnp.float32)
            for p in range(subs):
                for k in range(0, NB, piece):
                    cosines, sines = lag[0, :, k : k + piece], lag[1, :, k : k + piece]

                    def spread(at):
                        first = at // piece * chip + p * mine
                        out = jnp.broadcast_to(pack[first : first + 1], (hb, piece))
                        ids = lax.broadcasted_iota(jnp.int32, (hb, piece), 0) % mine
                        for v in range(1, mine):
                            out = jnp.where(ids == v, pack[first + v : first + v + 1], out)
                        return out

                    re, im = spread(k), spread(NB + k)
                    rc, rs, ic, js = re * cosines, re * sines, im * cosines, im * sines
                    at_re = slice(d * depth + k, d * depth + k + piece)
                    at_im = slice(d * depth + NB + k, d * depth + NB + k + piece)
                    rows[n, 2 * hb * p : 2 * hb * (p + 1), at_re] = jnp.concatenate(
                        [rc - js, rc + js], axis=0).astype(jnp.bfloat16)
                    rows[n, 2 * hb * p : 2 * hb * (p + 1), at_im] = jnp.concatenate(
                        [ic + rs, ic - rs], axis=0).astype(jnp.bfloat16)

    def correlate(n, i, alive):
        lags = lax.dot_general(rows[n], spectra[i], FAR, preferred_element_type=jnp.float32)
        lags = (lags * alive).astype(jnp.bfloat16)
        for p in range(subs):
            staged[n, i, p] = lags[2 * hb * p : 2 * hb * (p + 1)]

    def z_copy(n, i, p):
        return pltpu.make_async_remote_copy(
            src_ref=staged.at[n, i, p], dst_ref=far.at[n - 1, tile_of(i)],
            send_sem=z_send.at[n - 1, i, p], recv_sem=z_recv.at[n - 1, tile_of(i)],
            device_id={"chan": ring.giver(n), "sub": p}, device_id_type=MESH)

    def n_copy(n, i, u):
        there = lax.rem(sub_at + u, subs)
        return pltpu.make_async_remote_copy(
            src_ref=staged.at[n, i, there], dst_ref=near.at[n, tile_of(i)],
            send_sem=n_send.at[n, i, u - 1], recv_sem=n_recv.at[n, tile_of(i)],
            device_id={"sub": there}, device_id_type=MESH)

    for tile in range(tiles):
        live[tile] = mask[tile * TILE : (tile + 1) * TILE].reshape(1, TILE).astype(jnp.float32)

    def guarded(i, work):
        if (subs - 1) * per + i < tiles:
            work()
        else:
            pl.when(tile_of(i) < tiles)(work)

    def work_on(i):
        def work():
            if i:
                own_window(i)
            other_windows(i)
            alive = live[tile_of(i)]
            for n in range(1, slots):
                if i == 0:
                    fill(n)
                correlate(n, i, alive)
                for p in range(subs):
                    z_copy(n, i, p).start()
            if i == 0:
                fill(0)
            correlate(0, i, alive)
            for n in range(slots):
                for u in range(1, subs):
                    n_copy(n, i, u).start()
        guarded(i, work)

    for load in loads[2:]:
        load.wait()
    own_window(0)
    for i in range(per):
        work_on(i)

    split = hb // mine

    def place(out, offset, start, cells, gate, flipped):
        lanes = pl.ds(pl.multiple_of(start, TILE), TILE)
        cells = (cells.astype(jnp.float32) * gate).reshape(2 * split, mine, TILE)
        if flipped:
            out[offset, MAXLAG + 1 :, :, lanes] = cells[split + 1 : split + MAXLAG + 1]
            for lag_at in range(MAXLAG + 1):
                out[offset, MAXLAG - lag_at, :, lanes] = cells[lag_at]
        else:
            out[offset, MAXLAG:, :, lanes] = cells[: MAXLAG + 1]
            for lag_at in range(1, MAXLAG + 1):
                out[offset, MAXLAG - lag_at, :, lanes] = cells[split + lag_at]

    def receiver_cells(tile, read):
        for offset in range(OFFS):
            owner = lax.rem(block_at + 2 * blocks - offset + REACH, blocks)
            gate = pairs[owner, offset].astype(jnp.float32)
            place(fwd, offset, tile * TILE, read(ring.source_slot(offset)), gate, False)
        gate = pairs[block_at, REACH].astype(jnp.float32)
        place(back, REACH, tile * TILE, read(0), gate, True)

    for i in range(per):
        guarded(i, lambda i=i: receiver_cells(tile_of(i), lambda n: staged[n, i, sub_at]))
    for u in range(1, subs):
        there = lax.rem(sub_at + subs - u, subs)
        for i in range(per):
            def take(i=i, there=there):
                tile = there * per + i
                for n in range(slots):
                    pltpu.make_async_remote_copy(
                        src_ref=staged.at[n, i, 0], dst_ref=near.at[n, tile],
                        send_sem=n_send.at[n, i, 0], recv_sem=n_recv.at[n, tile],
                        device_id={"sub": there}, device_id_type=MESH).wait_recv()
                receiver_cells(tile, lambda n: near[n, tile])
            if (subs - 1) * per + i < tiles:
                take()
            else:
                pl.when(there * per + i < tiles)(take)

    for i, o in order:
        tile = o * per + i
        for n in range(1, slots):
            pltpu.make_async_remote_copy(
                src_ref=staged.at[n, i, 0], dst_ref=far.at[n - 1, tile],
                send_sem=z_send.at[n - 1, i, 0], recv_sem=z_recv.at[n - 1, tile],
                device_id={"chan": ring.giver(n)}, device_id_type=MESH).wait_recv()
        for offset in range(OFFS):
            if offset != REACH:
                gate = pairs[block_at, offset].astype(jnp.float32)
                cells = far[ring.receiver_slot(offset) - 1, tile]
                place(back, offset, tile * TILE, cells, gate, True)

    for copies in x_copies:
        for copy in copies:
            copy.wait_send()
    for copy in s_copies.values():
        copy.wait_send()
    for i in range(per):
        def drain(i=i):
            for n in range(slots):
                for p in range(subs):
                    if n:
                        z_copy(n, i, p).wait_send()
                for u in range(1, subs):
                    n_copy(n, i, u).wait_send()
        guarded(i, drain)


def write_out(fwd, back, fwd_out, back_out, sems):
    copies = []
    for offset in range(OFFS):
        for k, (here, there) in enumerate([(fwd, fwd_out), (back, back_out)]):
            copies.append(pltpu.make_async_copy(here.at[offset], there.at[offset], sems.at[k, offset]))
    for copy in copies:
        copy.start()
    for copy in copies:
        copy.wait()


def on_device(traces, channel_mask, smooth_width, source_phase, pair_list):
    windows, channels, samples = traces.shape
    subs = lax.axis_size("sub")
    wins = lax.axis_size("win")
    blocks = lax.axis_size("chan")
    mine = VS // (wins * subs)
    tiles = channels // TILE
    per = -(-tiles // subs)
    slots = len(block_keys(blocks))
    hb = half_rows(mine)
    chip = mine * subs
    depth = 2 * NB
    pack = (16, depth * chip // 16)
    vmem = pl.BlockSpec(memory_space=pltpu.VMEM)
    hbm = pl.BlockSpec(memory_space=pltpu.HBM)
    smem = pl.BlockSpec(memory_space=pltpu.SMEM)
    dma = pltpu.SemaphoreType.DMA
    half_type, full_type = jnp.bfloat16, jnp.float32
    stack = jax.ShapeDtypeStruct((OFFS, LAGS, mine, channels), full_type)
    stacks = pl.pallas_call(
        functools.partial(kernel, wins, subs, mine, tiles),
        out_shape=[stack, stack],
        in_specs=[smem, smem, hbm, vmem, vmem, hbm, hbm],
        out_specs=[vmem, vmem],
        scratch_shapes=[
            pltpu.VMEM((samples, depth), half_type),
            pltpu.VMEM((2, hb, NB), full_type),
            pltpu.VMEM((NB, NB), half_type),
            pltpu.VMEM((SPAN, samples), half_type),
            pltpu.VMEM((per, TILE, samples), half_type),
            pltpu.VMEM((max(wins - 1, 1), per, TILE, samples), half_type),
            pltpu.VMEM((per, TILE, wins * depth), half_type),
            pltpu.VMEM((slots, subs * 2 * hb, wins * depth), half_type),
            pltpu.VMEM((slots, per, subs, 2 * hb, TILE), half_type),
            pltpu.VMEM((slots, tiles, 2 * hb, TILE), half_type),
            pltpu.VMEM((slots - 1, tiles, 2 * hb, TILE), half_type),
            pltpu.VMEM((tiles, 1, TILE), full_type),
            pltpu.VMEM((VS, depth), full_type),
            pltpu.VMEM((wins,) + pack, full_type),
            pltpu.VMEM(pack, half_type),
            pltpu.VMEM((wins,) + pack, half_type),
            pltpu.VMEM((slots, wins) + pack, half_type),
            dma((3 + per,)),
            dma((per, subs, wins - 1)), dma((per, wins - 1, subs)),
            dma((slots, wins)), dma((slots, wins)),
            dma((slots, per, subs - 1)), dma((slots, tiles)),
            dma((slots - 1, per, subs)), dma((slots - 1, tiles)),
        ],
        compiler_params=pltpu.CompilerParams(
            collective_id=0, has_side_effects=True, vmem_limit_bytes=36 * 2**20
        ),
        name="stacks",
    )(*[
        pltpu.with_memory_space_constraint(operand, pltpu.HBM)
        for operand in (
            source_phase,
            pair_list,
            traces.reshape(channels, samples),
            channel_mask,
            smooth_width.reshape(1, NB),
            dft_columns(samples),
            lag_rows(samples, mine, (NB * windows * wins) ** (-0.5)),
        )
    ])
    stacks = pl.pallas_call(
        write_out,
        out_shape=[stack, stack],
        in_specs=[vmem, vmem],
        out_specs=[hbm, hbm],
        scratch_shapes=[dma((2, OFFS))],
        compiler_params=pltpu.CompilerParams(vmem_limit_bytes=16 * 2**20),
        name="write_out",
    )(*stacks)
    return tuple(jnp.transpose(cells, (2, 0, 1, 3)) for cells in stacks)


def solution(mesh):
    in_specs = (
        P(("groups", "win"), "chan", None),
        P(("groups", "chan")),
        P(),
        P("groups"),
        P("groups", None),
    )
    out_specs = (
        P(("win", "sub"), None, None, ("groups", "chan")),
        P(("groups", "chan", "win", "sub"), None, None, None),
    )
    return jax.shard_map(
        on_device, mesh=mesh, in_specs=in_specs, out_specs=out_specs, check_vma=False
    )
```

```python
import functools
import math

import jax
import jax.numpy as jnp
import numpy as np
from jax import lax
from jax.experimental import pallas as pl
from jax.experimental.pallas import tpu as pltpu
from jax.sharding import PartitionSpec as P

NB = 512
MAXLAG = 50
LAGS = 2 * MAXLAG + 1
STRIDE = 8
REACH = 2
VS = 8
OFFS = 2 * REACH + 1
FLOOR = 0.25
TILE = 128
SPAN = 64
MESH = pl.DeviceIdType.MESH
FAR = (((1,), (1,)), ((), ()))


def dft_columns(samples):
    phases = np.arange(samples)[:, None] * np.arange(NB)[None, :] % samples
    angles = phases * (2.0 * math.pi / samples)
    return jnp.asarray(np.concatenate([np.cos(angles), -np.sin(angles)], axis=1), jnp.bfloat16)


def half_rows(mine):
    return -(-(MAXLAG + 1) * mine // 8) * 8


def lag_rows(samples, mine, factor):
    lags = np.arange(half_rows(mine)) // mine
    angles = (lags[:, None] * np.arange(NB) % samples) * (2.0 * math.pi / samples)
    return jnp.asarray(np.stack([np.cos(angles), np.sin(angles)]) * factor, jnp.float32)


def block_keys(blocks):
    keys = [0]
    for offset in range(OFFS):
        key = (offset - REACH) % blocks
        if key not in keys:
            keys.append(key)
    return keys


class Ring:
    def __init__(self, blocks, at):
        self.blocks, self.at = blocks, at
        self.keys = block_keys(blocks)
        self.paired = blocks == 4
        self.slots = len(self.keys)

    def taker(self, slot):
        if self.paired:
            odd = self.at % 2
            return [self.at, (self.at + 2) % 4, 3 - self.at, self.at + 1 - 2 * odd][slot]
        return lax.rem(self.at + self.keys[slot], self.blocks)

    def giver(self, slot):
        if self.paired:
            return self.taker(slot)
        return lax.rem(self.at + self.blocks - self.keys[slot], self.blocks)

    def source_slot(self, offset):
        step = offset - REACH
        if self.paired and step % 2:
            odd = self.at % 2
            return 3 - odd if step == -1 else 2 + odd
        return self.keys.index(step % self.blocks)

    def receiver_slot(self, offset):
        step = offset - REACH
        if self.paired and step % 2:
            odd = self.at % 2
            return 2 + odd if step == -1 else 3 - odd
        return self.keys.index(step % self.blocks)


def kernel(wins, subs, mine, tiles, phase_ref, pairs, traces, mask, widths, dft_hbm, lag_hbm,
           fwd, back,
           dft, lag, weights, span_raw, raw, other_raw, spectra, rows, staged, near, far,
           live, picked, flat, own_pack, packs, got,
           l_sem, x_send, x_recv, s_send, s_recv, n_send, n_recv, z_send, z_recv,
           ready):
    samples = traces.shape[1]
    blocks = lax.axis_size("chan")
    block_at = lax.axis_index("chan")
    win_at = lax.axis_index("win")
    sub_at = lax.axis_index("sub")
    ring = Ring(blocks, block_at)
    slots = ring.slots
    per = -(-tiles // subs)
    chip = mine * subs
    hb = half_rows(mine)
    depth = 2 * NB

    def turned(d):
        return lax.rem(win_at + d, wins)

    barrier = pltpu.get_barrier_semaphore()
    last = subs - 1
    for d in range(wins):
        greet_last = functools.partial(
            pl.semaphore_signal, barrier, inc=1, device_id={"win": turned(d), "sub": last}, device_id_type=MESH)
        if d:
            greet_last()
        else:
            pl.when(sub_at != last)(greet_last)
    for n in range(slots):
        for d in range(wins):
            where = {"chan": ring.taker(n), "win": turned(d), "sub": 0}
            greet_first = functools.partial(
                pl.semaphore_signal, barrier, inc=1, device_id=where, device_id_type=MESH)
            if (n, d) != (0, 0):
                greet_first()
            else:
                pl.when(sub_at != 0)(greet_first)

    def tile_of(i):
        return sub_at * per + i

    loads = [
        pltpu.make_async_copy(traces.at[:SPAN], span_raw, l_sem.at[0]),
        pltpu.make_async_copy(dft_hbm, dft, l_sem.at[1]),
    ]
    for i in range(per):
        start = pl.multiple_of(jnp.minimum(tile_of(i), tiles - 1) * TILE, TILE)
        loads.append(pltpu.make_async_copy(traces.at[pl.ds(start, TILE)], raw.at[i], l_sem.at[2 + i]))
    loads.append(pltpu.make_async_copy(lag_hbm, lag, l_sem.at[2 + per]))
    for load in loads:
        load.start()

    width_row = widths[...].astype(jnp.float32)
    at = lax.broadcasted_iota(jnp.int32, (NB, NB), 0)
    to = lax.broadcasted_iota(jnp.int32, (NB, NB), 1)
    close = jnp.abs(at - to).astype(jnp.float32) <= width_row
    weights[...] = jnp.where(close, 1.0, 0.0).astype(jnp.bfloat16)
    bins = lax.broadcasted_iota(jnp.int32, (1, NB), 1).astype(jnp.float32)
    inside = jnp.minimum(bins + width_row, NB - 1.0) - jnp.maximum(bins - width_row, 0.0) + 1.0
    share = 1.0 / inside
    floor = FLOOR * samples**0.5

    def whiten(cut):
        both = jnp.dot(cut, dft[...], preferred_element_type=jnp.float32)
        re, im = both[:, :NB], both[:, NB:]
        amplitude = jnp.sqrt(re * re + im * im)
        high = amplitude.astype(jnp.bfloat16)
        low = (amplitude - high.astype(jnp.float32)).astype(jnp.bfloat16)
        total = jnp.dot(high, weights[...], preferred_element_type=jnp.float32)
        total = total + jnp.dot(low, weights[...], preferred_element_type=jnp.float32)
        gain = 1.0 / jnp.maximum(total * share, floor)
        return (re * gain).astype(jnp.bfloat16), (im * gain).astype(jnp.bfloat16)

    order = [(i, o) for i in range(per) for o in range(subs) if o * per + i < tiles]

    def x_copy(i, o, d):
        start = pl.multiple_of((o * per + i) * TILE, TILE)
        return pltpu.make_async_remote_copy(
            src_ref=traces.at[pl.ds(start, TILE)], dst_ref=other_raw.at[d - 1, i],
            send_sem=x_send.at[i, o, d - 1], recv_sem=x_recv.at[i, d - 1],
            device_id={"win": turned(d), "sub": o}, device_id_type=MESH)

    @pl.when(sub_at == last)
    def _():
        pl.semaphore_wait(barrier, wins * subs - 1)
        for i, o in order:
            for d in range(1, wins):
                x_copy(i, o, d).start()

    loads[0].wait()
    loads[1].wait()
    span_re, span_im = whiten(span_raw[...])
    phase = phase_ref[block_at]
    row_ids = lax.broadcasted_iota(jnp.int32, (VS, SPAN), 0)
    lane_ids = lax.broadcasted_iota(jnp.int32, (VS, SPAN), 1)
    alive = mask[:SPAN].reshape(1, SPAN).astype(jnp.float32)
    picker = jnp.where(lane_ids == phase + STRIDE * row_ids, alive, 0.0).astype(jnp.bfloat16)
    picked[:, :NB] = jnp.dot(picker, span_re, preferred_element_type=jnp.float32)
    picked[:, NB:] = jnp.dot(picker, span_im, preferred_element_type=jnp.float32)
    piece = packs.shape[-1]
    pieces = depth // piece
    for w in range(wins):
        for j in range(pieces):
            flat[w, j * chip : (j + 1) * chip, :] = picked[
                w * chip : (w + 1) * chip, j * piece : (j + 1) * piece]
    packs[...] = flat[...].astype(jnp.bfloat16)
    own_pack[...] = packs[win_at]
    for tile in range(tiles):
        live[tile] = mask[tile * TILE : (tile + 1) * TILE].reshape(1, TILE).astype(jnp.float32)
    @pl.when(sub_at == 0)
    def _():
        pl.semaphore_wait(barrier, slots * wins * subs - 1)
        for u in range(1, subs):
            pl.semaphore_signal(ready, inc=1, device_id={"sub": u}, device_id_type=MESH)

    @pl.when(sub_at != 0)
    def _():
        pl.semaphore_wait(ready, 1)

    def s_copy(n, d, u):
        where = {"chan": ring.taker(n), "win": turned(d)}
        if d:
            where["sub"] = u
        return pltpu.make_async_remote_copy(
            src_ref=packs.at[turned(d)], dst_ref=got.at[n, d],
            send_sem=s_send.at[n, d, u], recv_sem=s_recv.at[n, d],
            device_id=where, device_id_type=MESH)

    def over_x(act):
        @pl.when(sub_at == 0)
        def _():
            for n in list(range(1, slots)) + [0]:
                for d in range(1, wins):
                    for u in range(subs):
                        act(s_copy(n, d, u))

    for n in range(1, slots):
        s_copy(n, 0, 0).start()
    over_x(lambda copy: copy.start())
    def own_window(i):
        re, im = whiten(raw[i])
        spectra[i, :, :NB] = re
        spectra[i, :, NB:depth] = im

    def other_windows(i):
        for d in range(1, wins):
            x_copy(i, 0, d).wait_recv()
            re, im = whiten(other_raw[d - 1, i])
            spectra[i, :, d * depth : d * depth + NB] = re
            spectra[i, :, d * depth + NB : (d + 1) * depth] = im

    def lay_rows(pack, p, put):
        for k in range(0, NB, piece):
            cosines, sines = lag[0, :, k : k + piece], lag[1, :, k : k + piece]

            def spread(at):
                first = at // piece * chip + p * mine
                out = jnp.broadcast_to(pack[first : first + 1], (hb, piece))
                ids = lax.broadcasted_iota(jnp.int32, (hb, piece), 0) % mine
                for v in range(1, mine):
                    out = jnp.where(ids == v, pack[first + v : first + v + 1], out)
                return out

            re, im = spread(k), spread(NB + k)
            rc, rs, ic, js = re * cosines, re * sines, im * cosines, im * sines
            put(k, jnp.concatenate([rc - js, rc + js], axis=0).astype(jnp.bfloat16))
            put(NB + k, jnp.concatenate([ic + rs, ic - rs], axis=0).astype(jnp.bfloat16))

    def fill(n):
        for d in range(wins):
            if (n, d) == (0, 0):
                pack = own_pack[...].astype(jnp.float32)
            else:
                s_copy(n, d, 0).wait_recv()
                pack = got[n, d].astype(jnp.float32)
            for p in range(subs):
                def put(k, cells, d=d, p=p):
                    rows[n, 2 * hb * p : 2 * hb * (p + 1), d * depth + k : d * depth + k + piece] = cells
                lay_rows(pack, p, put)

    def correlate(n, i, alive):
        lags = lax.dot_general(rows[n], spectra[i], FAR, preferred_element_type=jnp.float32)
        lags = (lags * alive).astype(jnp.bfloat16)
        for p in range(subs):
            staged[n, i, p] = lags[2 * hb * p : 2 * hb * (p + 1)]

    def z_copy(n, i, p):
        return pltpu.make_async_remote_copy(
            src_ref=staged.at[n, i, p], dst_ref=far.at[n - 1, tile_of(i)],
            send_sem=z_send.at[n - 1, i, p], recv_sem=z_recv.at[n - 1, tile_of(i)],
            device_id={"chan": ring.giver(n), "sub": p}, device_id_type=MESH)

    def n_copy(n, i, u):
        there = lax.rem(sub_at + u, subs)
        return pltpu.make_async_remote_copy(
            src_ref=staged.at[n, i, there], dst_ref=near.at[n, tile_of(i)],
            send_sem=n_send.at[n, i, u - 1], recv_sem=n_recv.at[n, tile_of(i)],
            device_id={"sub": there}, device_id_type=MESH)

    def guarded(i, work):
        if (subs - 1) * per + i < tiles:
            work()
        else:
            pl.when(tile_of(i) < tiles)(work)

    def in_turn(first, second, i):
        first(i)
        second(i)

    def prepare(i):
        own_window(i)
        other_windows(i)

    def work_far(i):
        alive = live[tile_of(i)]
        for n in range(1, slots):
            if i == 0:
                fill(n)
            correlate(n, i, alive)
            for p in range(subs):
                z_copy(n, i, p).start()

    def work_near(i):
        correlate(0, i, live[tile_of(i)])
        for n in range(slots):
            for u in range(1, subs):
                n_copy(n, i, u).start()

    for load in loads[2 : 3 + per]:
        load.wait()
    prepare(0)
    if per > 1:
        guarded(1, lambda: own_window(1))
    work_far(0)
    if per > 1:
        guarded(1, lambda: in_turn(other_windows, work_far, 1))
    for i in range(2, per):
        guarded(i, lambda i=i: in_turn(prepare, work_far, i))
    fill(0)
    for i in range(per):
        guarded(i, lambda i=i: work_near(i))
    split = hb // mine

    def place(out, offset, start, cells, gate, flipped):
        lanes = pl.ds(pl.multiple_of(start, TILE), TILE)
        cells = (cells.astype(jnp.float32) * gate).reshape(2 * split, mine, TILE)
        if flipped:
            out[offset, MAXLAG + 1 :, :, lanes] = cells[split + 1 : split + MAXLAG + 1]
            for lag_at in range(MAXLAG + 1):
                out[offset, MAXLAG - lag_at, :, lanes] = cells[lag_at]
        else:
            out[offset, MAXLAG:, :, lanes] = cells[: MAXLAG + 1]
            for lag_at in range(1, MAXLAG + 1):
                out[offset, MAXLAG - lag_at, :, lanes] = cells[split + lag_at]

    def receiver_cells(tile, read):
        for offset in range(OFFS):
            owner = lax.rem(block_at + 2 * blocks - offset + REACH, blocks)
            gate = pairs[owner, offset].astype(jnp.float32)
            place(fwd, offset, tile * TILE, read(ring.source_slot(offset)), gate, False)
        gate = pairs[block_at, REACH].astype(jnp.float32)
        place(back, REACH, tile * TILE, read(0), gate, True)

    for i in range(per):
        guarded(i, lambda i=i: receiver_cells(tile_of(i), lambda n: staged[n, i, sub_at]))
    for u in range(1, subs):
        there = lax.rem(sub_at + subs - u, subs)
        for i in range(per):
            def take(i=i, there=there):
                tile = there * per + i
                for n in range(slots):
                    pltpu.make_async_remote_copy(
                        src_ref=staged.at[n, i, 0], dst_ref=near.at[n, tile],
                        send_sem=n_send.at[n, i, 0], recv_sem=n_recv.at[n, tile],
                        device_id={"sub": there}, device_id_type=MESH).wait_recv()
                receiver_cells(tile, lambda n: near[n, tile])
            if (subs - 1) * per + i < tiles:
                take()
            else:
                pl.when(there * per + i < tiles)(take)

    for i, o in order:
        tile = o * per + i
        for n in range(1, slots):
            pltpu.make_async_remote_copy(
                src_ref=staged.at[n, i, 0], dst_ref=far.at[n - 1, tile],
                send_sem=z_send.at[n - 1, i, 0], recv_sem=z_recv.at[n - 1, tile],
                device_id={"chan": ring.giver(n)}, device_id_type=MESH).wait_recv()
        for offset in range(OFFS):
            if offset != REACH:
                gate = pairs[block_at, offset].astype(jnp.float32)
                cells = far[ring.receiver_slot(offset) - 1, tile]
                place(back, offset, tile * TILE, cells, gate, True)

    @pl.when(sub_at == last)
    def _():
        for i, o in order:
            for d in range(1, wins):
                x_copy(i, o, d).wait_send()

    for n in range(1, slots):
        s_copy(n, 0, 0).wait_send()
    over_x(lambda copy: copy.wait_send())
    for i in range(per):
        def drain(i=i):
            for n in range(slots):
                for u in range(1, subs):
                    n_copy(n, i, u).wait_send()
            for n in range(1, slots):
                for p in range(subs):
                    z_copy(n, i, p).wait_send()
        guarded(i, drain)


def write_out(fwd, back, fwd_out, back_out, sems):
    copies = []
    for offset in range(OFFS):
        for k, (here, there) in enumerate([(fwd, fwd_out), (back, back_out)]):
            copies.append(pltpu.make_async_copy(here.at[offset], there.at[offset], sems.at[k, offset]))
    for copy in copies:
        copy.start()
    for copy in copies:
        copy.wait()


def on_device(traces, channel_mask, smooth_width, source_phase, pair_list):
    windows, channels, samples = traces.shape
    subs = lax.axis_size("sub")
    wins = lax.axis_size("win")
    blocks = lax.axis_size("chan")
    mine = VS // (wins * subs)
    tiles = channels // TILE
    per = -(-tiles // subs)
    slots = len(block_keys(blocks))
    hb = half_rows(mine)
    chip = mine * subs
    depth = 2 * NB
    pack = (16, depth * chip // 16)
    vmem = pl.BlockSpec(memory_space=pltpu.VMEM)
    hbm = pl.BlockSpec(memory_space=pltpu.HBM)
    smem = pl.BlockSpec(memory_space=pltpu.SMEM)
    dma = pltpu.SemaphoreType.DMA
    half_type, full_type = jnp.bfloat16, jnp.float32
    stack = jax.ShapeDtypeStruct((OFFS, LAGS, mine, channels), full_type)
    stacks = pl.pallas_call(
        functools.partial(kernel, wins, subs, mine, tiles),
        out_shape=[stack, stack],
        in_specs=[smem, smem, hbm, vmem, vmem, hbm, hbm],
        out_specs=[vmem, vmem],
        scratch_shapes=[
            pltpu.VMEM((samples, depth), half_type),
            pltpu.VMEM((2, hb, NB), full_type),
            pltpu.VMEM((NB, NB), half_type),
            pltpu.VMEM((SPAN, samples), half_type),
            pltpu.VMEM((per, TILE, samples), half_type),
            pltpu.VMEM((wins - 1, per, TILE, samples), half_type),
            pltpu.VMEM((per, TILE, wins * depth), half_type),
            pltpu.VMEM((slots, subs * 2 * hb, wins * depth), half_type),
            pltpu.VMEM((slots, per, subs, 2 * hb, TILE), half_type),
            pltpu.VMEM((slots, tiles, 2 * hb, TILE), half_type),
            pltpu.VMEM((slots - 1, tiles, 2 * hb, TILE), half_type),
            pltpu.VMEM((tiles, 1, TILE), full_type),
            pltpu.VMEM((VS, depth), full_type),
            pltpu.VMEM((wins,) + pack, full_type),
            pltpu.VMEM(pack, half_type),
            pltpu.VMEM((wins,) + pack, half_type),
            pltpu.VMEM((slots, wins) + pack, half_type),
            dma((3 + per,)),
            dma((per, subs, wins - 1)), dma((per, wins - 1)),
            dma((slots, wins, subs)), dma((slots, wins)),
            dma((slots, per, subs - 1)), dma((slots, tiles)),
            dma((slots - 1, per, subs)), dma((slots - 1, tiles)),
            pltpu.SemaphoreType.REGULAR,
        ],
        compiler_params=pltpu.CompilerParams(
            collective_id=0, has_side_effects=True, vmem_limit_bytes=36 * 2**20
        ),
        name="stacks",
    )(*[
        pltpu.with_memory_space_constraint(operand, pltpu.HBM)
        for operand in (
            source_phase,
            pair_list,
            traces.reshape(channels, samples),
            channel_mask,
            smooth_width.reshape(1, NB),
            dft_columns(samples),
            lag_rows(samples, mine, (NB * windows * wins) ** (-0.5)),
        )
    ])
    stacks = pl.pallas_call(
        write_out,
        out_shape=[stack, stack],
        in_specs=[vmem, vmem],
        out_specs=[hbm, hbm],
        scratch_shapes=[dma((2, OFFS))],
        compiler_params=pltpu.CompilerParams(vmem_limit_bytes=16 * 2**20),
        name="write_out",
    )(*stacks)
    return tuple(jnp.transpose(cells, (2, 0, 1, 3)) for cells in stacks)


def solution(mesh):
    in_specs = (
        P(("groups", "win"), "chan", None),
        P(("groups", "chan")),
        P(),
        P("groups"),
        P("groups", None),
    )
    out_specs = (
        P(("win", "sub"), None, None, ("groups", "chan")),
        P(("groups", "chan", "win", "sub"), None, None, None),
    )
    return jax.shard_map(
        on_device, mesh=mesh, in_specs=in_specs, out_specs=out_specs, check_vma=False
    )
```

```python
import functools
import math

import jax
import jax.numpy as jnp
import numpy as np
from jax import lax
from jax.experimental import pallas as pl
from jax.experimental.pallas import tpu as pltpu
from jax.sharding import PartitionSpec as P

NB = 512
MAXLAG = 50
LAGS = 2 * MAXLAG + 1
STRIDE = 8
REACH = 2
VS = 8
OFFS = 2 * REACH + 1
FLOOR = 0.25
TILE = 128
SPAN = 64
MESH = pl.DeviceIdType.MESH
FAR = (((1,), (1,)), ((), ()))


def dft_columns(samples):
    phases = np.arange(samples)[:, None] * np.arange(NB)[None, :] % samples
    angles = phases * (2.0 * math.pi / samples)
    return jnp.asarray(np.concatenate([np.cos(angles), -np.sin(angles)], axis=1), jnp.bfloat16)


def half_rows(mine):
    return -(-(MAXLAG + 1) * mine // 8) * 8


def lag_rows(samples, mine, factor):
    lags = np.arange(half_rows(mine)) // mine
    angles = (lags[:, None] * np.arange(NB) % samples) * (2.0 * math.pi / samples)
    return jnp.asarray(np.stack([np.cos(angles), np.sin(angles)]) * factor, jnp.float32)


def block_keys(blocks):
    keys = [0]
    for offset in range(OFFS):
        key = (offset - REACH) % blocks
        if key not in keys:
            keys.append(key)
    return keys


class Ring:
    def __init__(self, blocks, at):
        self.blocks, self.at = blocks, at
        self.keys = block_keys(blocks)
        self.paired = blocks == 4
        self.slots = len(self.keys)

    def taker(self, slot):
        if self.paired:
            odd = self.at % 2
            return [self.at, (self.at + 2) % 4, 3 - self.at, self.at + 1 - 2 * odd][slot]
        return lax.rem(self.at + self.keys[slot], self.blocks)

    def giver(self, slot):
        if self.paired:
            return self.taker(slot)
        return lax.rem(self.at + self.blocks - self.keys[slot], self.blocks)

    def source_slot(self, offset):
        step = offset - REACH
        if self.paired and step % 2:
            odd = self.at % 2
            return 3 - odd if step == -1 else 2 + odd
        return self.keys.index(step % self.blocks)

    def receiver_slot(self, offset):
        step = offset - REACH
        if self.paired and step % 2:
            odd = self.at % 2
            return 2 + odd if step == -1 else 3 - odd
        return self.keys.index(step % self.blocks)


def kernel(wins, subs, mine, tiles, phase_ref, pairs, traces, mask, widths, dft_hbm, lag_hbm,
           fwd, back,
           dft, lag, weights, span_raw, raw, other_raw, spectra, rows, staged, near, far,
           live, picked, flat, own_pack, packs, got,
           l_sem, x_send, x_recv, s_send, s_recv, n_send, n_recv, z_send, z_recv,
           ready):
    samples = traces.shape[1]
    blocks = lax.axis_size("chan")
    block_at = lax.axis_index("chan")
    win_at = lax.axis_index("win")
    sub_at = lax.axis_index("sub")
    ring = Ring(blocks, block_at)
    slots = ring.slots
    per = -(-tiles // subs)
    chip = mine * subs
    hb = half_rows(mine)
    depth = 2 * NB

    def turned(d):
        return lax.rem(win_at + d, wins)

    barrier = pltpu.get_barrier_semaphore()
    last = subs - 1
    for d in range(wins):
        greet_last = functools.partial(
            pl.semaphore_signal, barrier, inc=1, device_id={"win": turned(d), "sub": last}, device_id_type=MESH)
        if d:
            greet_last()
        else:
            pl.when(sub_at != last)(greet_last)
    for n in range(slots):
        for d in range(wins):
            where = {"chan": ring.taker(n), "win": turned(d), "sub": 0}
            greet_first = functools.partial(
                pl.semaphore_signal, barrier, inc=1, device_id=where, device_id_type=MESH)
            if (n, d) != (0, 0):
                greet_first()
            else:
                pl.when(sub_at != 0)(greet_first)

    def tile_of(i):
        return sub_at * per + i

    loads = [
        pltpu.make_async_copy(traces.at[:SPAN], span_raw, l_sem.at[0]),
        pltpu.make_async_copy(dft_hbm, dft, l_sem.at[1]),
    ]
    for i in range(per):
        start = pl.multiple_of(jnp.minimum(tile_of(i), tiles - 1) * TILE, TILE)
        loads.append(pltpu.make_async_copy(traces.at[pl.ds(start, TILE)], raw.at[i], l_sem.at[2 + i]))
    loads.append(pltpu.make_async_copy(lag_hbm, lag, l_sem.at[2 + per]))
    for load in loads:
        load.start()

    width_row = widths[...].astype(jnp.float32)
    at = lax.broadcasted_iota(jnp.int32, (NB, NB), 0)
    to = lax.broadcasted_iota(jnp.int32, (NB, NB), 1)
    close = jnp.abs(at - to).astype(jnp.float32) <= width_row
    weights[...] = jnp.where(close, 1.0, 0.0).astype(jnp.bfloat16)
    bins = lax.broadcasted_iota(jnp.int32, (1, NB), 1).astype(jnp.float32)
    inside = jnp.minimum(bins + width_row, NB - 1.0) - jnp.maximum(bins - width_row, 0.0) + 1.0
    share = 1.0 / inside
    floor = FLOOR * samples**0.5

    def whiten(cut):
        both = jnp.dot(cut, dft[...], preferred_element_type=jnp.float32)
        re, im = both[:, :NB], both[:, NB:]
        amplitude = jnp.sqrt(re * re + im * im)
        high = amplitude.astype(jnp.bfloat16)
        low = (amplitude - high.astype(jnp.float32)).astype(jnp.bfloat16)
        total = jnp.dot(high, weights[...], preferred_element_type=jnp.float32)
        total = total + jnp.dot(low, weights[...], preferred_element_type=jnp.float32)
        gain = 1.0 / jnp.maximum(total * share, floor)
        return (re * gain).astype(jnp.bfloat16), (im * gain).astype(jnp.bfloat16)

    order = [(i, o) for i in range(per) for o in range(subs) if o * per + i < tiles]

    def x_copy(i, o, d):
        start = pl.multiple_of((o * per + i) * TILE, TILE)
        return pltpu.make_async_remote_copy(
            src_ref=traces.at[pl.ds(start, TILE)], dst_ref=other_raw.at[d - 1, i],
            send_sem=x_send.at[i, o, d - 1], recv_sem=x_recv.at[i, d - 1],
            device_id={"win": turned(d), "sub": o}, device_id_type=MESH)

    @pl.when(sub_at == last)
    def _():
        pl.semaphore_wait(barrier, wins * subs - 1)
        for i, o in order:
            for d in range(1, wins):
                x_copy(i, o, d).start()

    loads[0].wait()
    loads[1].wait()
    span_re, span_im = whiten(span_raw[...])
    phase = phase_ref[block_at]
    row_ids = lax.broadcasted_iota(jnp.int32, (VS, SPAN), 0)
    lane_ids = lax.broadcasted_iota(jnp.int32, (VS, SPAN), 1)
    alive = mask[:SPAN].reshape(1, SPAN).astype(jnp.float32)
    picker = jnp.where(lane_ids == phase + STRIDE * row_ids, alive, 0.0).astype(jnp.bfloat16)
    picked[:, :NB] = jnp.dot(picker, span_re, preferred_element_type=jnp.float32)
    picked[:, NB:] = jnp.dot(picker, span_im, preferred_element_type=jnp.float32)
    piece = packs.shape[-1]
    pieces = depth // piece
    for w in range(wins):
        for j in range(pieces):
            flat[w, j * chip : (j + 1) * chip, :] = picked[
                w * chip : (w + 1) * chip, j * piece : (j + 1) * piece]
    packs[...] = flat[...].astype(jnp.bfloat16)
    own_pack[...] = packs[win_at]
    for tile in range(tiles):
        live[tile] = mask[tile * TILE : (tile + 1) * TILE].reshape(1, TILE).astype(jnp.float32)
    @pl.when(sub_at == 0)
    def _():
        pl.semaphore_wait(barrier, slots * wins * subs - 1)
        for u in range(1, subs):
            pl.semaphore_signal(ready, inc=1, device_id={"sub": u}, device_id_type=MESH)

    @pl.when(sub_at != 0)
    def _():
        pl.semaphore_wait(ready, 1)

    def s_copy(n, d, u):
        where = {"chan": ring.taker(n), "win": turned(d)}
        if d:
            where["sub"] = u
        return pltpu.make_async_remote_copy(
            src_ref=packs.at[turned(d)], dst_ref=got.at[n, d],
            send_sem=s_send.at[n, d, u], recv_sem=s_recv.at[n, d],
            device_id=where, device_id_type=MESH)

    def over_x(act):
        @pl.when(sub_at == 0)
        def _():
            for n in list(range(1, slots)) + [0]:
                for d in range(1, wins):
                    for u in range(subs):
                        act(s_copy(n, d, u))

    for n in range(1, slots):
        s_copy(n, 0, 0).start()
    over_x(lambda copy: copy.start())
    def own_window(i):
        re, im = whiten(raw[i])
        spectra[i, :, :NB] = re
        spectra[i, :, NB:depth] = im

    def other_windows(i):
        for d in range(1, wins):
            x_copy(i, 0, d).wait_recv()
            re, im = whiten(other_raw[d - 1, i])
            spectra[i, :, d * depth : d * depth + NB] = re
            spectra[i, :, d * depth + NB : (d + 1) * depth] = im

    row_source = lax.broadcasted_iota(jnp.int32, (hb, piece), 0) & (mine - 1)

    def lay_rows(pack, p, put):
        for k in range(0, NB, piece):
            cosines, sines = lag[0, :, k : k + piece], lag[1, :, k : k + piece]

            def spread(at):
                first = at // piece * chip + p * mine
                out = jnp.broadcast_to(pack[first : first + 1], (hb, piece))
                for v in range(1, mine):
                    out = jnp.where(row_source == v, pack[first + v : first + v + 1], out)
                return out

            re, im = spread(k), spread(NB + k)
            rc, rs, ic, js = re * cosines, re * sines, im * cosines, im * sines
            put(k, jnp.concatenate([rc - js, rc + js], axis=0).astype(jnp.bfloat16))
            put(NB + k, jnp.concatenate([ic + rs, ic - rs], axis=0).astype(jnp.bfloat16))

    def fill(n):
        for d in range(wins):
            if (n, d) == (0, 0):
                pack = own_pack[...].astype(jnp.float32)
            else:
                s_copy(n, d, 0).wait_recv()
                pack = got[n, d].astype(jnp.float32)
            for p in range(subs):
                def put(k, cells, d=d, p=p):
                    rows[n, 2 * hb * p : 2 * hb * (p + 1), d * depth + k : d * depth + k + piece] = cells
                lay_rows(pack, p, put)

    def correlate(n, i, alive):
        lags = lax.dot_general(rows[n], spectra[i], FAR, preferred_element_type=jnp.float32)
        lags = (lags * alive).astype(jnp.bfloat16)
        for p in range(subs):
            staged[n, i, p] = lags[2 * hb * p : 2 * hb * (p + 1)]

    def z_copy(n, i, p):
        return pltpu.make_async_remote_copy(
            src_ref=staged.at[n, i, p], dst_ref=far.at[n - 1, tile_of(i)],
            send_sem=z_send.at[n - 1, i, p], recv_sem=z_recv.at[n - 1, tile_of(i)],
            device_id={"chan": ring.giver(n), "sub": p}, device_id_type=MESH)

    def n_copy(n, i, u):
        there = lax.rem(sub_at + u, subs)
        return pltpu.make_async_remote_copy(
            src_ref=staged.at[n, i, there], dst_ref=near.at[n, tile_of(i)],
            send_sem=n_send.at[n, i, u - 1], recv_sem=n_recv.at[n, tile_of(i)],
            device_id={"sub": there}, device_id_type=MESH)

    def guarded(i, work):
        if (subs - 1) * per + i < tiles:
            work()
        else:
            pl.when(tile_of(i) < tiles)(work)

    def in_turn(first, second, i):
        first(i)
        second(i)

    def prepare(i):
        own_window(i)
        other_windows(i)

    def work_far(i):
        alive = live[tile_of(i)]
        for n in range(1, slots):
            if i == 0:
                fill(n)
            correlate(n, i, alive)
            for p in range(subs):
                z_copy(n, i, p).start()

    def work_near(i):
        correlate(0, i, live[tile_of(i)])
        for n in range(slots):
            for u in range(1, subs):
                n_copy(n, i, u).start()

    for load in loads[2 : 3 + per]:
        load.wait()
    prepare(0)
    work_far(0)
    if per > 1:
        guarded(1, lambda: own_window(1))
    if per > 1:
        guarded(1, lambda: in_turn(other_windows, work_far, 1))
    for i in range(2, per):
        guarded(i, lambda i=i: in_turn(prepare, work_far, i))
    fill(0)
    for i in range(per):
        guarded(i, lambda i=i: work_near(i))
    split = hb // mine

    def place(out, offset, start, cells, gate, flipped):
        lanes = pl.ds(pl.multiple_of(start, TILE), TILE)
        cells = (cells.astype(jnp.float32) * gate).reshape(2 * split, mine, TILE)
        if flipped:
            out[offset, MAXLAG + 1 :, :, lanes] = cells[split + 1 : split + MAXLAG + 1]
            for lag_at in range(MAXLAG + 1):
                out[offset, MAXLAG - lag_at, :, lanes] = cells[lag_at]
        else:
            out[offset, MAXLAG:, :, lanes] = cells[: MAXLAG + 1]
            for lag_at in range(1, MAXLAG + 1):
                out[offset, MAXLAG - lag_at, :, lanes] = cells[split + lag_at]

    def receiver_cells(tile, read):
        for offset in range(OFFS):
            owner = lax.rem(block_at + 2 * blocks - offset + REACH, blocks)
            gate = pairs[owner, offset].astype(jnp.float32)
            place(fwd, offset, tile * TILE, read(ring.source_slot(offset)), gate, False)
        gate = pairs[block_at, REACH].astype(jnp.float32)
        place(back, REACH, tile * TILE, read(0), gate, True)

    for i in range(per):
        guarded(i, lambda i=i: receiver_cells(tile_of(i), lambda n: staged[n, i, sub_at]))
    for u in range(1, subs):
        there = lax.rem(sub_at + subs - u, subs)
        for i in range(per):
            def take(i=i, there=there):
                tile = there * per + i
                for n in range(slots):
                    pltpu.make_async_remote_copy(
                        src_ref=staged.at[n, i, 0], dst_ref=near.at[n, tile],
                        send_sem=n_send.at[n, i, 0], recv_sem=n_recv.at[n, tile],
                        device_id={"sub": there}, device_id_type=MESH).wait_recv()
                receiver_cells(tile, lambda n: near[n, tile])
            if (subs - 1) * per + i < tiles:
                take()
            else:
                pl.when(there * per + i < tiles)(take)

    for i, o in order:
        tile = o * per + i
        for n in range(1, slots):
            pltpu.make_async_remote_copy(
                src_ref=staged.at[n, i, 0], dst_ref=far.at[n - 1, tile],
                send_sem=z_send.at[n - 1, i, 0], recv_sem=z_recv.at[n - 1, tile],
                device_id={"chan": ring.giver(n)}, device_id_type=MESH).wait_recv()
        for offset in range(OFFS):
            if offset != REACH:
                gate = pairs[block_at, offset].astype(jnp.float32)
                cells = far[ring.receiver_slot(offset) - 1, tile]
                place(back, offset, tile * TILE, cells, gate, True)

    @pl.when(sub_at == last)
    def _():
        for i, o in order:
            for d in range(1, wins):
                x_copy(i, o, d).wait_send()

    for n in range(1, slots):
        s_copy(n, 0, 0).wait_send()
    over_x(lambda copy: copy.wait_send())
    for i in range(per):
        def drain(i=i):
            for n in range(slots):
                for u in range(1, subs):
                    n_copy(n, i, u).wait_send()
            for n in range(1, slots):
                for p in range(subs):
                    z_copy(n, i, p).wait_send()
        guarded(i, drain)


def write_out(fwd, back, fwd_out, back_out, sems):
    copies = []
    for offset in range(OFFS):
        for k, (here, there) in enumerate([(fwd, fwd_out), (back, back_out)]):
            copies.append(pltpu.make_async_copy(here.at[offset], there.at[offset], sems.at[k, offset]))
    for copy in copies:
        copy.start()
    for copy in copies:
        copy.wait()


def on_device(traces, channel_mask, smooth_width, source_phase, pair_list):
    windows, channels, samples = traces.shape
    subs = lax.axis_size("sub")
    wins = lax.axis_size("win")
    blocks = lax.axis_size("chan")
    mine = VS // (wins * subs)
    tiles = channels // TILE
    per = -(-tiles // subs)
    slots = len(block_keys(blocks))
    hb = half_rows(mine)
    chip = mine * subs
    depth = 2 * NB
    pack = (16, depth * chip // 16)
    vmem = pl.BlockSpec(memory_space=pltpu.VMEM)
    hbm = pl.BlockSpec(memory_space=pltpu.HBM)
    smem = pl.BlockSpec(memory_space=pltpu.SMEM)
    dma = pltpu.SemaphoreType.DMA
    half_type, full_type = jnp.bfloat16, jnp.float32
    stack = jax.ShapeDtypeStruct((OFFS, LAGS, mine, channels), full_type)
    stacks = pl.pallas_call(
        functools.partial(kernel, wins, subs, mine, tiles),
        out_shape=[stack, stack],
        in_specs=[smem, smem, hbm, vmem, vmem, hbm, hbm],
        out_specs=[vmem, vmem],
        scratch_shapes=[
            pltpu.VMEM((samples, depth), half_type),
            pltpu.VMEM((2, hb, NB), full_type),
            pltpu.VMEM((NB, NB), half_type),
            pltpu.VMEM((SPAN, samples), half_type),
            pltpu.VMEM((per, TILE, samples), half_type),
            pltpu.VMEM((wins - 1, per, TILE, samples), half_type),
            pltpu.VMEM((per, TILE, wins * depth), half_type),
            pltpu.VMEM((slots, subs * 2 * hb, wins * depth), half_type),
            pltpu.VMEM((slots, per, subs, 2 * hb, TILE), half_type),
            pltpu.VMEM((slots, tiles, 2 * hb, TILE), half_type),
            pltpu.VMEM((slots - 1, tiles, 2 * hb, TILE), half_type),
            pltpu.VMEM((tiles, 1, TILE), full_type),
            pltpu.VMEM((VS, depth), full_type),
            pltpu.VMEM((wins,) + pack, full_type),
            pltpu.VMEM(pack, half_type),
            pltpu.VMEM((wins,) + pack, half_type),
            pltpu.VMEM((slots, wins) + pack, half_type),
            dma((3 + per,)),
            dma((per, subs, wins - 1)), dma((per, wins - 1)),
            dma((slots, wins, subs)), dma((slots, wins)),
            dma((slots, per, subs - 1)), dma((slots, tiles)),
            dma((slots - 1, per, subs)), dma((slots - 1, tiles)),
            pltpu.SemaphoreType.REGULAR,
        ],
        compiler_params=pltpu.CompilerParams(
            collective_id=0, has_side_effects=True, vmem_limit_bytes=36 * 2**20
        ),
        name="stacks",
    )(*[
        pltpu.with_memory_space_constraint(operand, pltpu.HBM)
        for operand in (
            source_phase,
            pair_list,
            traces.reshape(channels, samples),
            channel_mask,
            smooth_width.reshape(1, NB),
            dft_columns(samples),
            lag_rows(samples, mine, (NB * windows * wins) ** (-0.5)),
        )
    ])
    stacks = pl.pallas_call(
        write_out,
        out_shape=[stack, stack],
        in_specs=[vmem, vmem],
        out_specs=[hbm, hbm],
        scratch_shapes=[dma((2, OFFS))],
        compiler_params=pltpu.CompilerParams(vmem_limit_bytes=16 * 2**20),
        name="write_out",
    )(*stacks)
    return tuple(jnp.transpose(cells, (2, 0, 1, 3)) for cells in stacks)


def solution(mesh):
    in_specs = (
        P(("groups", "win"), "chan", None),
        P(("groups", "chan")),
        P(),
        P("groups"),
        P("groups", None),
    )
    out_specs = (
        P(("win", "sub"), None, None, ("groups", "chan")),
        P(("groups", "chan", "win", "sub"), None, None, None),
    )
    return jax.shard_map(
        on_device, mesh=mesh, in_specs=in_specs, out_specs=out_specs, check_vma=False
    )
```
